32 devices in a mesh: lat: 4 (over x, core), lon: 8 (over z, y).
Axes of the slice: x: 2, y: 2, z: 4, core: 2. Of those that a mesh axis runs over, the one named last changes fastest.
Arguments:
- nodes: bfloat16 [4, 8, 384, 512], P('lat', 'lon'), may hold values from -6 to 6
- edges: bfloat16 [4, 8, 3072, 512], P('lat', 'lon'), may hold values from -6 to 6
- senders: int32 [4, 8, 3072], P('lat', 'lon'), may hold values from 0 to 511, as said below
- receivers: int32 [4, 8, 3072], P('lat', 'lon'), may hold values from 0 to 383
- edge_count: int32 [4, 8], P('lat', 'lon'), may hold values from 1536 to 3072, as said below
- halo_send: int32 [4, 8, 4, 24], P('lat', 'lon'), may hold values from 0 to 383
- long_need: int32 [4, 8, 32, 1], P('lat', 'lon'), may hold values from 0 to 1
- node_cot: bfloat16 [4, 8, 384, 512], P('lat', 'lon'), may hold values from -6 to 6
- edge_cot: bfloat16 [4, 8, 3072, 512], P('lat', 'lon'), may hold values from -6 to 6
- e_w1: bfloat16 [1536, 512], replicated, may hold values from -0.15625 to 0.15625
- e_b1: float32 [512], replicated, may hold values from -3 to 3
- e_w2: bfloat16 [512, 512], replicated, may hold values from -0.25 to 0.25
- e_gain: float32 [512], replicated, may hold values from 0.25 to 1.75
- n_w1: bfloat16 [1024, 512], replicated, may hold values from -0.1875 to 0.1875
- n_b1: float32 [512], replicated, may hold values from -3 to 3
- n_w2: bfloat16 [512, 512], replicated, may hold values from -0.25 to 0.25
- n_gain: float32 [512], replicated, may hold values from 0.25 to 1.75
Outputs:
- new_nodes: bfloat16 [4, 8, 384, 512], P('lat', 'lon')
- new_edges: bfloat16 [4, 8, 3072, 512], P('lat', 'lon')
- node_grad: float32 [4, 8, 384, 512], P('lat', 'lon')
- edge_grad: float32 [4, 8, 3072, 512], P('lat', 'lon')
- e_w1_grad: float32 [1536, 512], P(('lat', 'lon'))
- e_b1_grad: float32 [512], P(('lat', 'lon'))
- e_w2_grad: float32 [512, 512], P(('lat', 'lon'))
- e_gain_grad: float32 [512], P(('lat', 'lon'))
- n_w1_grad: float32 [1024, 512], P(('lat', 'lon'))
- n_b1_grad: float32 [512], P(('lat', 'lon'))
- n_w2_grad: float32 [512, 512], P(('lat', 'lon'))
- n_gain_grad: float32 [512], P(('lat', 'lon'))
The draws below stay inside these ranges and needn't reach their ends.
Inputs may be any that keep to these rules, and one draw needn't show every extreme that they name: `senders`: entries below 384 are a region's own nodes, the next 96 the four neighbour blocks, the rest the coarse rows; the third block is never named in the first band and the fourth never in the last. The first three edge slots of region r name the coarse rows of regions r + 1, r - 1 and r + 16 in flat order, counted round. `edge_count`: some region has all 3072 slots live. `long_need`: A region's coarse nodes are its first 2 rows.
All inputs are finite; a program needn't handle non-finite values.
Results may differ from the reference program's by a relative error of at most 0.009.
Values may be sent and summed in bfloat16 or wider, within the bound.
A program may use at most 192 MiB of HBM per device.

```python
import jax
import jax.numpy as jnp
from jax import lax

D = 512
H = 512
NODE_DEV = 384
HALO = 24
COARSE = 2
LONG_SLOT = 1
E_DEV = 3072
N_LAT = 4
N_LON = 8
DEVICES = 32


def draw_senders(key, part):
    keys = jax.random.split(jax.random.fold_in(key, 11), 5)
    shape = (N_LAT, N_LON, E_DEV)
    regions = N_LAT * N_LON
    kind = jax.random.randint(keys[0], shape, 0, 100)
    local = jax.random.randint(keys[1], shape, 0, NODE_DEV)
    block = jax.random.randint(keys[2], shape, 0, 4)
    band = jnp.arange(N_LAT).reshape(N_LAT, 1, 1)
    block = jnp.where((block == 2) & (band == 0), 0, block)
    block = jnp.where((block == 3) & (band == N_LAT - 1), 1, block)
    halo = NODE_DEV + block * HALO + jax.random.randint(keys[3], shape, 0, HALO)
    far = NODE_DEV + 4 * HALO + jax.random.randint(keys[4], shape, 0, regions * LONG_SLOT)
    picked = jnp.where(kind < 80, local, jnp.where(kind < 97, halo, far))
    flat_index = jnp.arange(regions, dtype=jnp.int32).reshape(N_LAT, N_LON, 1)
    offsets = jnp.array([1, regions - 1, regions // 2], dtype=jnp.int32).reshape(1, 1, 3)
    source = (flat_index + offsets) % regions
    fixed_rows = NODE_DEV + 4 * HALO + source * LONG_SLOT
    slot = jnp.arange(E_DEV, dtype=jnp.int32).reshape(1, 1, E_DEV)
    padded = jnp.concatenate([fixed_rows, jnp.zeros((N_LAT, N_LON, E_DEV - 3), jnp.int32)], axis=2)
    return jnp.where(slot < 3, padded, picked).astype(jnp.int32)


def draw_edge_count(key, part):
    keys = jax.random.split(jax.random.fold_in(key, 23), 2)
    counts = jax.random.randint(keys[0], (N_LAT * N_LON,), E_DEV // 2, E_DEV + 1)
    fullest = jax.random.randint(keys[1], (), 0, N_LAT * N_LON)
    counts = jnp.where(jnp.arange(N_LAT * N_LON) == fullest, E_DEV, counts)
    return counts.reshape(N_LAT, N_LON).astype(jnp.int32)


def touch_ends(values, rng, least, top_value):
    longest = values.shape.index(max(values.shape))
    spots = []
    for shift in (0, 1):
        where = [jax.random.randint(jax.random.fold_in(rng, axis), (), 0, length) for axis, length in enumerate(values.shape)]
        where[longest] = (where[longest] + shift) % values.shape[longest]
        spots.append(tuple(where))
    return values.at[spots[0]].set(least).at[spots[1]].set(top_value)


def block_levels(own_key, extent, cuts, least, largest):
    level, own = 1.0, jax.random.fold_in(own_key, 6)
    for dim, blocks in cuts:
        steps = jnp.exp(jax.random.uniform(jax.random.fold_in(own, dim), (blocks,), jnp.float32, least / len(cuts), largest / len(cuts)))
        level = level * jnp.repeat(steps, extent[dim] // blocks).reshape([-1 if axis == dim else 1 for axis in range(len(extent))])
    return level


def noise(key, dims, scale, most, cuts=(), kind=jnp.bfloat16):
    values = scale * jax.random.normal(key, dims, jnp.float32)
    if cuts:
        values = values * block_levels(key, dims, cuts, -0.22, 0.18)
    return jnp.clip(values, -most, most).astype(kind)


def setup_inputs(seed: int = 0) -> dict:
    key_of = jax.random.split(jax.random.key(seed), 18)
    nodes = noise(key_of[0], (N_LAT, N_LON, NODE_DEV, D), 1.0, 6.0, ((0, 4), (1, 8)))
    edges = noise(key_of[1], (N_LAT, N_LON, E_DEV, D), 1.0, 6.0, ((0, 4), (1, 8)))
    senders = draw_senders(jax.random.fold_in(key_of[17], 71), 0)
    receivers = touch_ends(jax.random.randint(key_of[3], (N_LAT, N_LON, E_DEV), 0, NODE_DEV), jax.random.fold_in(key_of[3], 1), 0, NODE_DEV - 1).astype(jnp.int32)
    edge_count = draw_edge_count(jax.random.fold_in(key_of[17], 71), 0)
    halo_send = touch_ends(jax.random.randint(key_of[5], (N_LAT, N_LON, 4, HALO), 0, NODE_DEV), jax.random.fold_in(key_of[5], 1), 0, NODE_DEV - 1).astype(jnp.int32)
    long_need = touch_ends(jax.random.randint(key_of[6], (N_LAT, N_LON, DEVICES, LONG_SLOT), 0, COARSE), jax.random.fold_in(key_of[6], 1), 0, COARSE - 1).astype(jnp.int32)
    node_cot = noise(key_of[7], (N_LAT, N_LON, NODE_DEV, D), 1.0, 6.0, ((0, 4), (1, 8)))
    edge_cot = noise(key_of[8], (N_LAT, N_LON, E_DEV, D), 1.0, 6.0, ((0, 4), (1, 8)))
    e_w1 = noise(key_of[9], (3 * D, H), (3 * D) ** -0.5, 0.15625)
    e_b1 = noise(key_of[10], (H,), 0.5, 3.0, (), jnp.float32)
    e_w2 = noise(key_of[11], (H, D), H ** -0.5, 0.25)
    e_gain = jnp.clip(1.0 + 0.15 * jax.random.normal(key_of[12], (D,), jnp.float32), 0.25, 1.75)
    n_w1 = noise(key_of[13], (2 * D, H), (2 * D) ** -0.5, 0.1875)
    n_b1 = noise(key_of[14], (H,), 0.5, 3.0, (), jnp.float32)
    n_w2 = noise(key_of[15], (H, D), H ** -0.5, 0.25)
    n_gain = jnp.clip(1.0 + 0.15 * jax.random.normal(key_of[16], (D,), jnp.float32), 0.25, 1.75)
    return {"nodes": nodes, "edges": edges, "senders": senders, "receivers": receivers, "edge_count": edge_count, "halo_send": halo_send, "long_need": long_need, "node_cot": node_cot, "edge_cot": edge_cot, "e_w1": e_w1, "e_b1": e_b1, "e_w2": e_w2, "e_gain": e_gain, "n_w1": n_w1, "n_b1": n_b1, "n_w2": n_w2, "n_gain": n_gain}


EPS = 1e-05

def layer_norm(z, gain):
    mean = lax.optimization_barrier(jnp.mean(z, axis=-1, keepdims=True))
    centred = z - mean
    rstd = lax.rsqrt(lax.optimization_barrier(jnp.mean(centred * centred, axis=-1, keepdims=True)) + EPS)
    normed = centred * rstd
    return (normed * gain, normed, rstd)

def transposed(left, right):
    return lax.dot_general(left, right, (((0,), (0,)), ((), ())), preferred_element_type=jnp.float32)

def mlp_forward(parts, w_first, b_first, w_second, gain):
    joined = jnp.concatenate(parts, axis=1)
    z_first = jnp.dot(joined, w_first, preferred_element_type=jnp.float32) + b_first
    active = jax.nn.silu(z_first).astype(jnp.bfloat16)
    z_second = jnp.dot(active, w_second, preferred_element_type=jnp.float32)
    result, normed, rstd = layer_norm(z_second, gain)
    return (result, (z_first, active, normed, rstd))

def mlp_backward(parts, saved, grad_out, w_first, w_second, gain):
    z_first, active, normed, rstd = saved
    gain_grad = lax.optimization_barrier(jnp.sum(grad_out * normed, axis=0))
    scaled = grad_out * gain
    g_second = rstd * (scaled - lax.optimization_barrier(jnp.mean(scaled, axis=-1, keepdims=True)) - normed * lax.optimization_barrier(jnp.mean(scaled * normed, axis=-1, keepdims=True)))
    g_second = g_second.astype(jnp.bfloat16)
    second_grad = transposed(active, g_second)
    g_active = jnp.dot(g_second, w_second.T, preferred_element_type=jnp.float32)
    sigma = jax.nn.sigmoid(z_first)
    g_first = (g_active * sigma * (1.0 + z_first * (1.0 - sigma))).astype(jnp.bfloat16)
    bias_grad = lax.optimization_barrier(jnp.sum(g_first, axis=0, dtype=jnp.float32))
    joined = jnp.concatenate(parts, axis=1)
    first_grad = transposed(joined, g_first)
    g_input = jnp.dot(g_first, w_first.T, preferred_element_type=jnp.float32)
    return (g_input, (first_grad, bias_grad, second_grad, gain_grad))

def device_pass(table, nodes_l, edges_l, snd, rcv, count, node_cot_l, edge_cot_l, weights):
    e_w1, e_b1, e_w2, e_gain, n_w1, n_b1, n_w2, n_gain = weights
    width = nodes_l.shape[1]
    node_n = nodes_l.shape[0]
    sent_rows = jnp.take(table, snd, axis=0)
    recv_rows = jnp.take(nodes_l, rcv, axis=0)
    edge_parts = (edges_l, sent_rows, recv_rows)
    edge_out, edge_saved = mlp_forward(edge_parts, e_w1, e_b1, e_w2, e_gain)
    alive = jnp.arange(edges_l.shape[0]) < count
    live = alive.astype(jnp.float32)[:, None]
    new_edges = (edges_l + live * edge_out).astype(jnp.bfloat16)
    recv_table = ((rcv[None, :] == jnp.arange(node_n)[:, None]) & alive[None, :]).astype(jnp.bfloat16)
    aggregate = jnp.dot(recv_table, new_edges, preferred_element_type=jnp.float32).astype(jnp.bfloat16)
    node_parts = (nodes_l, aggregate)
    node_out, node_saved = mlp_forward(node_parts, n_w1, n_b1, n_w2, n_gain)
    new_nodes = (nodes_l + node_out).astype(jnp.bfloat16)
    node_up = node_cot_l.astype(jnp.float32)
    g_node_in, node_grads = mlp_backward(node_parts, node_saved, node_up, n_w1, n_w2, n_gain)
    g_aggregate = g_node_in[:, width:]
    g_new_edges = edge_cot_l.astype(jnp.float32) + live * jnp.take(g_aggregate, rcv, axis=0)
    g_edge_in, edge_grads = mlp_backward(edge_parts, edge_saved, live * g_new_edges, e_w1, e_w2, e_gain)
    g_edge_in = g_edge_in.astype(jnp.bfloat16)
    edge_grad = g_new_edges + g_edge_in[:, :width]
    node_local = node_up + g_node_in[:, :width] + jnp.dot(recv_table, g_edge_in[:, 2 * width:], preferred_element_type=jnp.float32)
    send_table = (snd[None, :] == jnp.arange(table.shape[0])[:, None]).astype(jnp.bfloat16)
    sender_grad = jnp.dot(send_table, g_edge_in[:, width:2 * width], preferred_element_type=jnp.float32)
    return (new_nodes, new_edges, edge_grad, node_local, sender_grad, edge_grads + node_grads)

def pick_rows(source, rows):
    return jnp.take(source, rows, axis=0)

def add_rows(rows, values, node_n, width):
    return jnp.zeros((node_n, width), jnp.float32).at[rows].add(values)

def reference(nodes, edges, senders, receivers, edge_count, halo_send, long_need, node_cot, edge_cot, e_w1, e_b1, e_w2, e_gain, n_w1, n_b1, n_w2, n_gain):
    lat_n, lon_n, node_n, width = nodes.shape
    devices = lat_n * lon_n
    halo_n = halo_send.shape[3]
    slot_n = long_need.shape[3]
    sent = jax.vmap(jax.vmap(pick_rows))(nodes, halo_send)
    zero_band = jnp.zeros_like(sent[:1, :, 2])
    block_east = jnp.roll(sent[:, :, 0], 1, axis=1)
    block_west = jnp.roll(sent[:, :, 1], -1, axis=1)
    block_north = jnp.concatenate([zero_band, sent[:-1, :, 2]], axis=0)
    block_south = jnp.concatenate([sent[1:, :, 3], zero_band], axis=0)
    halo = jnp.stack([block_east, block_west, block_north, block_south], axis=2).reshape(lat_n, lon_n, 4 * halo_n, width)
    coarse = nodes[:, :, :COARSE].reshape(devices * COARSE, width)
    far_ids = (jnp.arange(devices, dtype=jnp.int32)[:, None] * COARSE + long_need).reshape(lat_n, lon_n, devices * slot_n)
    far = jnp.take(coarse, far_ids, axis=0)
    table = jnp.concatenate([nodes, halo, far], axis=2).reshape(devices, -1, width)
    weights = (e_w1, e_b1, e_w2, e_gain, n_w1, n_b1, n_w2, n_gain)

    def flat(array):
        return array.reshape((devices,) + array.shape[2:])
    inputs = (table, flat(nodes), flat(edges), flat(senders), flat(receivers), edge_count.reshape(devices), flat(node_cot), flat(edge_cot))
    init = tuple((jnp.zeros(weight.shape, jnp.float32) for weight in weights))

    def step(carry, item):
        new_nodes, new_edges, edge_grad, node_local, sender_grad, grads = device_pass(*item, weights)
        carry = tuple((total + grad for total, grad in zip(carry, grads)))
        return (carry, (new_nodes, new_edges, edge_grad, node_local, sender_grad))
    sums, outputs = lax.scan(step, init, inputs)
    new_nodes, new_edges, edge_grad, node_local, sender_grad = outputs
    sender_grad = sender_grad.reshape(lat_n, lon_n, -1, width)
    halo_grad = sender_grad[:, :, node_n:node_n + 4 * halo_n].reshape(lat_n, lon_n, 4, halo_n, width)
    far_grad = sender_grad[:, :, node_n + 4 * halo_n:]
    zero_grad = jnp.zeros_like(halo_grad[:1, :, 2])
    back_east = jnp.roll(halo_grad[:, :, 0], -1, axis=1)
    back_west = jnp.roll(halo_grad[:, :, 1], 1, axis=1)
    back_north = jnp.concatenate([halo_grad[1:, :, 2], zero_grad], axis=0)
    back_south = jnp.concatenate([zero_grad, halo_grad[:-1, :, 3]], axis=0)
    back = jnp.stack([back_east, back_west, back_north, back_south], axis=2).reshape(lat_n, lon_n, 4 * halo_n, width)
    node_grad = node_local.reshape(lat_n, lon_n, node_n, width) + sender_grad[:, :, :node_n]
    returned = jax.vmap(jax.vmap(lambda rows, values: add_rows(rows, values, node_n, width)))(halo_send.reshape(lat_n, lon_n, 4 * halo_n), back)
    node_grad = node_grad + returned
    coarse_grad = jax.ops.segment_sum(far_grad.reshape(-1, width), far_ids.reshape(-1), num_segments=devices * COARSE)
    node_grad = node_grad.at[:, :, :COARSE].add(coarse_grad.reshape(lat_n, lon_n, COARSE, width))
    return (new_nodes.reshape(nodes.shape), new_edges.reshape(edges.shape), node_grad, edge_grad.reshape(edges.shape), sums[0], sums[1], sums[2], sums[3], sums[4], sums[5], sums[6], sums[7])
```

```python
import jax
import jax.numpy as jnp
from jax import lax
from jax.sharding import PartitionSpec as P

COARSE = 2


EPS = 1e-05


def shifted(block, axis, distance):
    devices = range(lax.axis_size(axis))
    route = [((i - distance) % len(devices), i) for i in devices]
    return lax.ppermute(block, axis, route)


def passed_along(value, axis, steps):
    count = lax.axis_size(axis)
    leading, last = (max(0, -steps), min(count, count - steps))
    return lax.ppermute(value, axis, [(source, source + steps) for source in range(leading, last)])


def layer_norm(z, gain):
    mean = jnp.mean(z, axis=-1, keepdims=True)
    centred = z - mean
    rstd = lax.rsqrt(jnp.mean(centred * centred, axis=-1, keepdims=True) + EPS)
    normed = centred * rstd
    return (normed * gain, normed, rstd)


def transposed(left, right):
    return lax.dot_general(
        left, right, (((0,), (0,)), ((), ())), preferred_element_type=jnp.float32
    )


def mlp_forward(parts, w_first, b_first, w_second, gain):
    width = parts[0].shape[1]
    z_first = b_first
    for number, piece in enumerate(parts):
        z_first = z_first + jnp.dot(
            piece,
            w_first[number * width : (number + 1) * width],
            preferred_element_type=jnp.float32,
        )
    active = jax.nn.silu(z_first).astype(jnp.bfloat16)
    z_second = jnp.dot(active, w_second, preferred_element_type=jnp.float32)
    result, normed, rstd = layer_norm(z_second, gain)
    return (result, (z_first, active, normed, rstd))


def mlp_backward(parts, saved, grad_out, w_first, w_second, gain):
    z_first, active, normed, rstd = saved
    gain_grad = jnp.sum(grad_out * normed, axis=0)
    scaled = grad_out * gain
    g_second = rstd * (
        scaled
        - jnp.mean(scaled, axis=-1, keepdims=True)
        - normed * jnp.mean(scaled * normed, axis=-1, keepdims=True)
    )
    g_second = g_second.astype(jnp.bfloat16)
    second_grad = transposed(active, g_second)
    g_active = jnp.dot(g_second, w_second.T, preferred_element_type=jnp.float32)
    sigma = jax.nn.sigmoid(z_first)
    g_first = (g_active * sigma * (1.0 + z_first * (1.0 - sigma))).astype(jnp.bfloat16)
    bias_grad = jnp.sum(g_first, axis=0, dtype=jnp.float32)
    first_grad = jnp.concatenate([transposed(piece, g_first) for piece in parts], axis=0)
    g_input = jnp.dot(g_first, w_first.T, preferred_element_type=jnp.float32)
    return (g_input, (first_grad, bias_grad, second_grad, gain_grad))


def shards(
    nodes,
    edges,
    senders,
    receivers,
    edge_count,
    halo_send,
    long_need,
    node_cot,
    edge_cot,
    e_w1,
    e_b1,
    e_w2,
    e_gain,
    n_w1,
    n_b1,
    n_w2,
    n_gain,
):
    nodes_l = nodes[0, 0]
    edges_l = edges[0, 0]
    snd = senders[0, 0]
    rcv = receivers[0, 0]
    count = edge_count[0, 0]
    rows_out = halo_send[0, 0]
    need = long_need[0, 0]
    node_n, width = nodes_l.shape
    halo_n = rows_out.shape[1]
    devices, slot_n = need.shape
    axes = ("lat", "lon")

    def exchange(value):
        return lax.all_to_all(value, axes, split_axis=0, concat_axis=0, tiled=True)

    def one_hot(ids, count, keep=None):
        hit = ids[:, None] == jnp.arange(count)[None, :]
        if keep is not None:
            hit = hit & keep[:, None]
        return hit.astype(jnp.bfloat16)

    def one_hot_t(ids, count, keep=None):
        hit = ids[None, :] == jnp.arange(count)[:, None]
        if keep is not None:
            hit = hit & keep[None, :]
        return hit.astype(jnp.bfloat16)

    def product(left, right):
        return jnp.dot(left, right, preferred_element_type=jnp.float32)

    sent = product(one_hot(rows_out.reshape(-1), node_n), nodes_l).astype(jnp.bfloat16)
    sent = sent.reshape(4, halo_n, width)
    from_east = shifted(sent[0], "lon", 1)
    from_west = shifted(sent[1], "lon", -1)
    from_north = passed_along(sent[2], "lat", 1)
    from_south = passed_along(sent[3], "lat", -1)
    coarse = exchange(jnp.broadcast_to(nodes_l[:COARSE][None], (devices, COARSE, width)))
    far = jnp.zeros((devices, slot_n, width), jnp.bfloat16)
    for c in range(COARSE):
        far = jnp.where((need == c)[:, :, None], coarse[:, c][:, None, :], far)
    far = far.reshape(devices * slot_n, width)
    table = jnp.concatenate([nodes_l, from_east, from_west, from_north, from_south, far], axis=0)
    table_n = table.shape[0]
    w_edge, w_send, w_recv = (e_w1[i * width : (i + 1) * width] for i in range(3))
    alive = jnp.arange(edges_l.shape[0]) < count
    live = alive.astype(jnp.float32)[:, None]
    z_edge = product(edges_l, w_edge) + e_b1
    p_recv = product(nodes_l, w_recv).astype(jnp.bfloat16)
    p_send = product(table, w_send).astype(jnp.bfloat16)
    picked = jnp.concatenate([p_send, p_recv], axis=0)
    columns = jnp.arange(table_n + node_n)[None, :]
    pick = (
        ((snd[:, None] == columns) | (rcv[:, None] + table_n == columns)) & alive[:, None]
    ).astype(jnp.bfloat16)
    z_first = z_edge + product(pick, picked)
    active = jax.nn.silu(z_first).astype(jnp.bfloat16)
    z_second = product(active, e_w2)
    edge_out, normed, rstd = layer_norm(z_second, e_gain)
    new_edges = (edges_l + live * edge_out).astype(jnp.bfloat16)
    recv_t = one_hot_t(rcv, node_n, alive)
    aggregate = product(recv_t, new_edges).astype(jnp.bfloat16)
    node_parts = (nodes_l, aggregate)
    node_out, node_saved = mlp_forward(node_parts, n_w1, n_b1, n_w2, n_gain)
    new_nodes = (nodes_l + node_out).astype(jnp.bfloat16)
    node_up = node_cot[0, 0].astype(jnp.float32)
    g_node_in, node_grads = mlp_backward(node_parts, node_saved, node_up, n_w1, n_w2, n_gain)
    n_first, n_bias, n_second, n_scale = node_grads
    g_aggregate = g_node_in[:, width:].astype(jnp.bfloat16)
    g_new_edges = edge_cot[0, 0].astype(jnp.float32) + product(
        one_hot(rcv, node_n, alive), g_aggregate
    )
    grad_out = live * g_new_edges
    e_scale = jnp.sum(grad_out * normed, axis=0)
    scaled = grad_out * e_gain
    g_second = rstd * (
        scaled
        - jnp.mean(scaled, axis=-1, keepdims=True)
        - normed * jnp.mean(scaled * normed, axis=-1, keepdims=True)
    )
    g_second = g_second.astype(jnp.bfloat16)
    e_second = transposed(active, g_second)

    def split(value):
        return value.astype(jnp.bfloat16).reshape(devices, -1, value.shape[-1])

    early = exchange(jnp.concatenate([split(n_first), split(n_second), split(e_second)], axis=1))
    g_active = product(g_second, e_w2.T)
    sigma = jax.nn.sigmoid(z_first)
    g_first = (g_active * sigma * (1.0 + z_first * (1.0 - sigma))).astype(jnp.bfloat16)
    e_bias = jnp.sum(g_first, axis=0, dtype=jnp.float32)
    rows = jnp.arange(table_n + node_n)[:, None]
    pick_t = (
        ((snd[None, :] == rows) | (rcv[None, :] + table_n == rows)) & alive[None, :]
    ).astype(jnp.bfloat16)
    spread = product(pick_t, g_first).astype(jnp.bfloat16)
    spread_send, spread_recv = spread[:table_n], spread[table_n:]
    e_first = jnp.concatenate(
        [
            transposed(edges_l, g_first),
            transposed(table, spread_send),
            transposed(nodes_l, spread_recv),
        ],
        axis=0,
    )
    late = exchange(split(e_first))
    sender_grad = product(spread_send, w_send.T)
    edge_grad = g_new_edges + product(g_first, w_edge.T)
    halo_part = sender_grad[node_n : node_n + 4 * halo_n].astype(jnp.bfloat16)
    to_east = shifted(halo_part[:halo_n], "lon", -1)
    to_west = shifted(halo_part[halo_n : 2 * halo_n], "lon", 1)
    to_north = passed_along(halo_part[2 * halo_n : 3 * halo_n], "lat", -1)
    to_south = passed_along(halo_part[3 * halo_n :], "lat", 1)
    far_grad = sender_grad[node_n + 4 * halo_n :].reshape(devices, slot_n, width)
    to_coarse = jnp.stack(
        [
            jnp.sum(jnp.where((need == c)[:, :, None], far_grad, 0.0), axis=1)
            for c in range(COARSE)
        ],
        axis=1,
    ).astype(jnp.bfloat16)
    vectors = jnp.concatenate(
        [v.reshape(devices, -1) for v in (e_bias, e_scale, n_bias, n_scale)], axis=1
    )
    high = vectors.astype(jnp.bfloat16)
    low = (vectors - high.astype(jnp.float32)).astype(jnp.bfloat16)
    extra = jnp.concatenate([high, low], axis=1)
    vector_n = vectors.shape[1]
    extra_rows = -(-extra.shape[1] // width)
    extra = jnp.pad(extra, ((0, 0), (0, extra_rows * width - extra.shape[1])))
    came = exchange(
        jnp.concatenate([to_coarse, extra.reshape(devices, extra_rows, width)], axis=1)
    ).astype(jnp.float32)
    came = jnp.sum(came, axis=0)
    coarse_grad = came[:COARSE]
    flat = came[COARSE:].reshape(-1)
    vector = (flat[:vector_n] + flat[vector_n : 2 * vector_n]).reshape(4, -1)
    returned = jnp.concatenate([to_east, to_west, to_north, to_south], axis=0)
    border_t = one_hot_t(rows_out.reshape(-1), node_n)
    node_grad = (
        node_up
        + g_node_in[:, :width]
        + product(spread_recv, w_recv.T)
        + sender_grad[:node_n]
        + product(border_t, returned)
    )
    node_grad = node_grad + jnp.pad(coarse_grad, ((0, node_n - COARSE), (0, 0)))
    early = jnp.sum(early.astype(jnp.float32), axis=0)
    late = jnp.sum(late.astype(jnp.float32), axis=0)
    n_one = n_first.shape[0] // devices
    n_two = n_one + n_second.shape[0] // devices
    sums = (
        late,
        vector[0],
        early[n_two:],
        vector[1],
        early[:n_one],
        vector[2],
        early[n_one:n_two],
        vector[3],
    )
    return (
        new_nodes[None, None],
        new_edges[None, None],
        node_grad[None, None],
        edge_grad[None, None],
        sums[0],
        sums[1],
        sums[2],
        sums[3],
        sums[4],
        sums[5],
        sums[6],
        sums[7],
    )


def solution(mesh):
    return jax.shard_map(
        shards,
        mesh=mesh,
        in_specs=(
            P("lat", "lon", None, None),
            P("lat", "lon", None, None),
            P("lat", "lon", None),
            P("lat", "lon", None),
            P("lat", "lon"),
            P("lat", "lon", None, None),
            P("lat", "lon", None, None),
            P("lat", "lon", None, None),
            P("lat", "lon", None, None),
            P(),
            P(),
            P(),
            P(),
            P(),
            P(),
            P(),
            P(),
        ),
        out_specs=(
            P("lat", "lon", None, None),
            P("lat", "lon", None, None),
            P("lat", "lon", None, None),
            P("lat", "lon", None, None),
            P(("lat", "lon"), None),
            P(("lat", "lon")),
            P(("lat", "lon"), None),
            P(("lat", "lon")),
            P(("lat", "lon"), None),
            P(("lat", "lon")),
            P(("lat", "lon"), None),
            P(("lat", "lon")),
        ),
        check_vma=False,
    )
```
